32 devices in a mesh: grp: 4 (over z), brick: 8 (over y, x, core).
Axes of the slice: x: 2, y: 2, z: 4, core: 2. Of those that a mesh axis runs over, the one named last changes fastest.
Arguments:
- store: bfloat16 [96, 256, 256], P(('grp', 'brick')), may hold values from -0.01171875 to 0.01171875
- crossing: int32 [32, 4], P('grp'), may hold values from 0 to 23, as said below
- phi: bfloat16 [32, 64, 16, 1024], P('grp', 'brick'), may hold values from -6 to 6
- rows_index: int32 [32, 4, 256], P(('grp', 'brick')), may hold values from 0 to 1023
- cols_index: int32 [32, 4, 256], P(('grp', 'brick')), may hold values from 0 to 1023
Outputs:
- hamiltonian: float32 [96, 256, 256], P(('grp', 'brick'))
The draws below stay inside these ranges and needn't reach their ends.
Inputs may be any that keep to these rules, and one draw needn't show every extreme that they name: `crossing`: each row lists 4 different blocks of its group; block k of a group is held by the device with brick index k // 3 of that group. A row names at most 1 block held by one device, and exactly 1 of some device.
All inputs are finite; a program needn't handle non-finite values.
Results may differ from the reference program's by a relative error of at most 0.0029.
Values may be sent and summed in bfloat16 or wider, within the bound.
A program may use at most 128 MiB of HBM per device.

```python
import math
import jax
import jax.numpy as jnp
from jax import lax

NF = 256
F = 1024
CAP = 1
OWN = 3
CX = 8
CY = 8
CZ = 16
NBLK = 4
BRICKS = 32
NX = 32
NY = 64
N_GRP = 4
N_BRICK = 8


def draw_crossing(key, part):

    def single_row(row_key):
        key_order, key_first, key_offset = jax.random.split(row_key, 3)
        items = N_BRICK * CAP
        position = jax.random.permutation(key_order, items).astype(jnp.int32)
        owner = jnp.arange(items, dtype=jnp.int32) // CAP
        first = jax.random.randint(key_first, (), 0, N_BRICK, dtype=jnp.int32)
        score = jnp.where(owner == first, -1, position)
        order = jnp.argsort(score, stable=True)[:NBLK].astype(jnp.int32)
        offsets = jax.random.randint(key_offset, (N_BRICK,), 0, OWN, dtype=jnp.int32)
        chosen_owner = order // CAP
        chosen_slot = order % CAP
        return (chosen_owner * OWN + (offsets[chosen_owner] + chosen_slot * (OWN // CAP)) % OWN).astype(jnp.int32)
    return jax.vmap(single_row)(jax.random.split(key, N_GRP * N_BRICK))


def set_ends(entries, own_key, low, high):
    dims = entries.shape
    spot = [jax.random.randint(jax.random.fold_in(own_key, axis), (), 0, dims[axis]) for axis in range(len(dims))]
    entries = entries.at[tuple(spot)].set(low)
    longest = dims.index(max(dims))
    spot[longest] = (spot[longest] + 1) % dims[longest]
    return entries.at[tuple(spot)].set(high)


def block_scale(own_key, shape, cuts, low, largest):
    level, own = 1.0, jax.random.fold_in(own_key, 6)
    for dim, parts in cuts:
        heights = jnp.exp(jax.random.uniform(jax.random.fold_in(own, dim), (parts,), jnp.float32, low / len(cuts), largest / len(cuts)))
        level = level * jnp.repeat(heights, shape[dim] // parts).reshape([-1 if axis == dim else 1 for axis in range(len(shape))])
    return level


def bell_draw(own_key, extent, scale, bound, cuts=(), kind=jnp.bfloat16):
    loudness = block_scale(own_key, extent, cuts, -0.22, 0.18) if cuts else 1.0
    array = jax.random.normal(own_key, extent, jnp.float32) * scale * loudness
    return jnp.minimum(jnp.maximum(array, -bound), bound).astype(kind)


def setup_inputs(seed: int = 0) -> dict:
    key_list = jax.random.split(jax.random.key(seed), 6)
    store = bell_draw(key_list[0], (BRICKS * OWN, NF, NF), (NBLK * NF * NF) ** -0.5, 0.01171875, ((0, 32),))
    crossing = draw_crossing(jax.random.fold_in(key_list[5], 71), 0)
    phi = bell_draw(key_list[2], (NX, NY, CZ, F), 1.0, 6.0, ((0, 4), (1, 8)))
    rows_index = set_ends(jax.random.randint(key_list[3], (BRICKS, NBLK, NF), 0, F), jax.random.fold_in(key_list[3], 1), 0, F - 1).astype(jnp.int32)
    cols_index = set_ends(jax.random.randint(key_list[4], (BRICKS, NBLK, NF), 0, F), jax.random.fold_in(key_list[4], 1), 0, F - 1).astype(jnp.int32)
    return {"store": store, "crossing": crossing, "phi": phi, "rows_index": rows_index, "cols_index": cols_index}


GRAD_WEIGHT = 0.5

def brick_table(phi, brick_id):
    group = brick_id // N_BRICK
    member = brick_id % N_BRICK
    zero = jnp.zeros((), jnp.int32)
    piece = lax.dynamic_slice(phi, ((group * CX).astype(jnp.int32), (member * CY).astype(jnp.int32), zero, zero), (CX, CY, CZ, F))
    return piece.reshape(CX * CY * CZ, F).T

def difference(field, axis):
    return (jnp.roll(field, -1, axis) - jnp.roll(field, 1, axis)) * 0.5

def potential_of(density):
    grad_x = difference(density, 0)
    grad_y = difference(density, 1)
    grad_z = difference(density, 2)
    sigma = grad_x * grad_x + grad_y * grad_y + grad_z * grad_z
    factor = 2.0 * GRAD_WEIGHT / (1.0 + sigma)
    diverge = difference(factor * grad_x, 0) + difference(factor * grad_y, 1) + difference(factor * grad_z, 2)
    return density / jnp.sqrt(1.0 + density * density) - diverge

def reference(store, crossing, phi, rows_index, cols_index):
    points = CX * CY * CZ
    dvol = 1.0 / math.sqrt(points)
    block_ids = jnp.arange(NBLK, dtype=jnp.int32)

    def global_ids(brick_id):
        return (brick_id // N_BRICK * (N_BRICK * OWN) + crossing[brick_id]).astype(jnp.int32)

    def collocate(brick_id):
        table = brick_table(phi, brick_id)
        ids = global_ids(brick_id)

        def single(index):
            left = table[rows_index[brick_id, index]]
            right = table[cols_index[brick_id, index]]
            product = jnp.dot(store[ids[index]], right, preferred_element_type=jnp.float32)
            return lax.optimization_barrier(jnp.sum(left.astype(jnp.float32) * product, axis=0))
        return lax.optimization_barrier(jnp.sum(lax.map(single, block_ids), axis=0))
    bricks_all = jnp.arange(N_GRP * N_BRICK, dtype=jnp.int32)
    dens = lax.map(collocate, bricks_all)
    density = dens.reshape(N_GRP, N_BRICK, CX, CY, CZ).transpose(0, 2, 1, 3, 4).reshape(N_GRP * CX, N_BRICK * CY, CZ)
    potential = potential_of(density)
    pot_bricks = potential.reshape(N_GRP, CX, N_BRICK, CY, CZ).transpose(0, 2, 1, 3, 4).reshape(N_GRP * N_BRICK, points)

    def integrate(total, brick_id):
        table = brick_table(phi, brick_id)
        ids = global_ids(brick_id)
        scaled = pot_bricks[brick_id] * dvol

        def single(index):
            left = table[rows_index[brick_id, index]]
            weighted = (table[cols_index[brick_id, index]].astype(jnp.float32) * scaled[None, :]).astype(jnp.bfloat16)
            return lax.dot_general(left, weighted, (((1,), (1,)), ((), ())), preferred_element_type=jnp.float32)
        partial_value = lax.map(single, block_ids)
        return (total.at[ids].add(partial_value), None)
    start = jnp.zeros((N_GRP * N_BRICK * OWN, NF, NF), jnp.float32)
    hamiltonian, unused = lax.scan(integrate, start, bricks_all)
    return hamiltonian
```

```python
import functools
import math

import jax
import jax.numpy as jnp
from jax import lax
from jax.experimental import pallas as pl
from jax.experimental.pallas import tpu as pltpu
from jax.sharding import PartitionSpec as P

GRAD_WEIGHT = 0.5
CORE, LOW, HIGH = 2, 2, 2
MESH = pl.DeviceIdType.MESH
NT = (((1,), (1,)), ((), ()))


def partner_of(bricks, brick, r):
    if bricks & (bricks - 1):
        return lax.rem(r - brick + bricks, bricks)
    other = brick
    for bit in range(bricks.bit_length() - 1):
        if r >> bit & 1:
            other = other + (1 << bit) * (1 - 2 * lax.rem(lax.div(brick, 1 << bit), 2))
    return other


def block_number(crossing_ref, own, whom, owner):
    number, taken = jnp.int32(0), jnp.int32(0)
    for j in range(crossing_ref.shape[0]):
        entry = crossing_ref[j, whom]
        hit = lax.div(entry, own) == owner
        number = jnp.where(hit, lax.rem(entry, own), number)
        taken = jnp.where(hit, 1, taken)
    return number, taken


def make_tabulate(rows_ref, cols_ref, phi_v, row_t, col_t):
    width, functions = row_t.shape[1], phi_v.shape[1]
    lane = lax.broadcasted_iota(jnp.int32, (width, 128), 1)

    def pick(index_ref, table_ref, j):
        index = jnp.broadcast_to(index_ref[0, pl.ds(j, 1), :], (128, width)).T
        onehot = jnp.concatenate(
            [
                jnp.where(index == lane + k * 128, 1.0, 0.0).astype(jnp.bfloat16)
                for k in range(functions // 128)
            ],
            axis=1,
        )
        table_ref[j] = lax.dot_general(
            onehot, phi_v[...], NT, preferred_element_type=jnp.float32
        ).astype(jnp.bfloat16)

    def tabulate(j, carry):
        pick(rows_ref, row_t, j)
        pick(cols_ref, col_t, j)
        return carry

    return tabulate


def scaled_potential(halo, size_z):
    tall, wide = halo.shape[2:]
    points = tall * wide
    field = jnp.concatenate(
        [jnp.concatenate([halo[i, k] for k in range(3)], axis=1) for i in range(3)], axis=0
    )
    rows, lanes = field.shape
    depth = lax.rem(lax.broadcasted_iota(jnp.int32, field.shape, 1), size_z)

    def along_x(f):
        return (pltpu.roll(f, rows - 1, 0) - pltpu.roll(f, 1, 0)) * 0.5

    def along_y(f):
        return (pltpu.roll(f, lanes - size_z, 1) - pltpu.roll(f, size_z, 1)) * 0.5

    def along_z(f):
        up = jnp.where(
            depth == size_z - 1, pltpu.roll(f, size_z - 1, 1), pltpu.roll(f, lanes - 1, 1)
        )
        down = jnp.where(depth == 0, pltpu.roll(f, lanes - size_z + 1, 1), pltpu.roll(f, 1, 1))
        return (up - down) * 0.5

    grad_x, grad_y, grad_z = along_x(field), along_y(field), along_z(field)
    sigma = grad_x * grad_x + grad_y * grad_y + grad_z * grad_z
    factor = 2.0 * GRAD_WEIGHT / (1.0 + sigma)
    diverge = along_x(factor * grad_x) + along_y(factor * grad_y) + along_z(factor * grad_z)
    centre = field[tall : 2 * tall, wide : 2 * wide]
    potential = centre / jnp.sqrt(1.0 + centre * centre) - diverge[
        tall : 2 * tall, wide : 2 * wide
    ]
    scaled = potential * (1.0 / math.sqrt(points))
    scaled = jnp.concatenate([scaled[x : x + 1, :] for x in range(tall)], axis=1)
    return scaled


def position_in(crossing_ref, own, whom, owner):
    where, taken = jnp.int32(0), jnp.int32(0)
    for j in range(crossing_ref.shape[0]):
        hit = lax.div(crossing_ref[j, whom], own) == owner
        where = jnp.where(hit, j, where)
        taken = jnp.where(hit, 1, taken)
    return where, taken


def kernel(
    groups, bricks, size_z,
    crossing_ref, rows_hbm, cols_hbm, store_hbm, phi_hbm, out_ref,
    rows_ref, cols_ref, store_v, phi_v, outgoing, incoming, row_t, col_t, dens, halo, back, landed,
    load_sem, send_sem, recv_sem, halo_send, halo_recv, back_send, back_recv,
):
    group = lax.axis_index("grp")
    brick = lax.axis_index("brick")
    own, width = store_v.shape[0], store_v.shape[1]
    blocks = crossing_ref.shape[0]
    points, functions = phi_v.shape
    tall, wide = dens.shape

    load_store = pltpu.make_async_copy(store_hbm, store_v, load_sem.at[0])
    load_phi = pltpu.make_async_copy(phi_hbm, phi_v, load_sem.at[1])
    load_rows = pltpu.make_async_copy(rows_hbm, rows_ref, load_sem.at[2])
    load_cols = pltpu.make_async_copy(cols_hbm, cols_ref, load_sem.at[3])
    load_store.start()
    load_phi.start()
    load_rows.start()
    load_cols.start()

    def member(offset):
        return lax.rem(brick + (offset % bricks), bricks)

    partner = functools.partial(partner_of, bricks, brick)
    order = sorted(range(1, bricks), key=lambda r: (r == 1, r & 1, bin(r >> 1).count("1")))

    def place(dg, db):
        return (lax.rem(group + (dg % groups), groups), member(db))

    around = [(dg, db) for dg in (-1, 0, 1) for db in (-1, 0, 1) if (dg, db) != (0, 0)]
    reached = {(0, r) for r in range(1, bricks)}
    reached |= {(dg % groups, db % bricks) for dg, db in around}
    reached = sorted(reached)
    barrier = pltpu.get_barrier_semaphore()
    for dg, db in reached:
        pl.semaphore_signal(barrier, inc=1, device_id=place(dg, db), device_id_type=MESH)

    position_of = functools.partial(position_in, crossing_ref, own, brick)

    load_store.wait()
    for r in order:
        number, _ = block_number(crossing_ref, own, partner(r), brick)
        outgoing[r] = store_v[number]
    number, _ = block_number(crossing_ref, own, brick, brick)
    incoming[0] = store_v[number]
    pl.semaphore_wait(barrier, len(reached))
    sends = []
    for r in order:
        copy = pltpu.make_async_remote_copy(
            src_ref=outgoing.at[r], dst_ref=incoming.at[r],
            send_sem=send_sem.at[r], recv_sem=recv_sem.at[r],
            device_id=(group, partner(r)), device_id_type=MESH,
        )
        copy.start()
        sends.append(copy)

    load_rows.wait()
    load_cols.wait()
    load_phi.wait()
    tabulate = make_tabulate(rows_ref, cols_ref, phi_v, row_t, col_t)
    lax.fori_loop(0, blocks, tabulate, 0)

    density = jnp.zeros((1, points), jnp.float32)
    for n, r in enumerate([0] + order):
        where, taken = position_of(partner(r) if r else brick)
        if n:
            sends[n - 1].wait()
        product = jnp.dot(incoming[r], col_t[where], preferred_element_type=jnp.float32)
        term = jnp.sum(row_t[where].astype(jnp.float32) * product, axis=0, keepdims=True)
        density = density + jnp.where(taken == 1, term, 0.0)
    for x in range(tall):
        dens[x : x + 1, :] = density[:, x * wide : (x + 1) * wide]
    halo[1, 1] = dens[...]
    exchange = []
    for n, (dg, db) in enumerate(around):
        copy = pltpu.make_async_remote_copy(
            src_ref=dens, dst_ref=halo.at[1 - dg, 1 - db],
            send_sem=halo_send.at[n], recv_sem=halo_recv.at[n],
            device_id=place(dg, db), device_id_type=MESH,
        )
        copy.start()
        exchange.append(copy)
    for copy in exchange:
        copy.wait()

    scaled = scaled_potential(halo, size_z)

    returns = []
    for r in order + [0]:
        where, _ = position_of(partner(r) if r else brick)
        weighted = (col_t[where].astype(jnp.float32) * scaled).astype(jnp.bfloat16)
        back[r] = lax.dot_general(
            row_t[where], weighted, NT, preferred_element_type=jnp.float32
        ).astype(jnp.bfloat16)
        if r:
            copy = pltpu.make_async_remote_copy(
                src_ref=back.at[r], dst_ref=landed.at[r],
                send_sem=back_send.at[r], recv_sem=back_recv.at[r],
                device_id=(group, partner(r)), device_id_type=MESH,
            )
            copy.start()
            returns.append(copy)
    for n, r in enumerate([0] + order):
        number, taken = block_number(crossing_ref, own, partner(r) if r else brick, brick)
        if n:
            returns[n - 1].wait()
        value = (landed if n else back)[r].astype(jnp.float32)
        for k in range(own):
            term = jnp.where((taken == 1) & (number == k), value, 0.0)
            out_ref[k] = out_ref[k] + term if n else term


def cube_kernel(
    groups, bricks, size_z,
    crossing_ref, rows_hbm, cols_hbm, store_hbm, phi_hbm, out_ref,
    rows_ref, cols_ref, store_v, phi_v, mate, picked, stage, incoming, row_t, col_t,
    dens, halo, back, kept, relay, sums, direct, mate_back, sums_back,
    load_sem, send_sem, recv_sem, ready, halo_send, halo_recv, back_send, back_recv,
):
    group = lax.axis_index("grp")
    brick = lax.axis_index("brick")
    own, width = store_v.shape[0], store_v.shape[1]
    half = width // 2
    points = phi_v.shape[0]
    blocks = crossing_ref.shape[0]
    tall, wide = dens.shape
    upper, lower = pl.ds(0, half), pl.ds(half, half)
    low, high = CORE, CORE * LOW
    partner = functools.partial(partner_of, bricks, brick)
    number_of = functools.partial(block_number, crossing_ref, own)

    loads = [
        pltpu.make_async_copy(source, target, load_sem.at[n])
        for n, (source, target) in enumerate(
            ((store_hbm, store_v), (rows_hbm, rows_ref), (cols_hbm, cols_ref), (phi_hbm, phi_v))
        )
    ]
    barrier = pltpu.get_barrier_semaphore()
    near = (1, low, low + 1, high, high + 1)

    def along_chain(semaphore):
        @pl.when(group > 0)
        def _():
            pl.semaphore_signal(
                semaphore, inc=1, device_id=(group - 1, brick), device_id_type=MESH
            )

        @pl.when(group < groups - 1)
        def _():
            pl.semaphore_signal(
                semaphore, inc=1, device_id=(group + 1, brick), device_id_type=MESH
            )

    links = jnp.where(group > 0, 1, 0) + jnp.where(group < groups - 1, 1, 0)
    for r in near:
        pl.semaphore_signal(barrier, inc=1, device_id=(group, partner(r)), device_id_type=MESH)
    along_chain(barrier)
    for load in loads:
        load.start()
    pl.semaphore_wait(barrier, len(near) + links)

    for r in near:
        pl.semaphore_signal(ready.at[0], inc=1, device_id=(group, partner(r)), device_id_type=MESH)

    def spread(n):
        if n >= groups:
            return
        pl.semaphore_wait(ready.at[n], links if n else len(near))
        if n + 1 < groups:
            along_chain(ready.at[n + 1])

    def sender(send, recv):
        def start(n, source, target, r):
            copy = pltpu.make_async_remote_copy(
                src_ref=source, dst_ref=target, send_sem=send.at[n], recv_sem=recv.at[n],
                device_id=(group, partner(r)), device_id_type=MESH,
            )
            copy.start()
            return copy
        return start

    give = sender(send_sem, recv_sem)
    sends = {}
    sends[0] = give(0, store_hbm.at[:, upper], stage.at[0], high)
    sends[1] = give(1, store_hbm.at[:, lower], stage.at[1], low)
    loads[0].wait()
    for n, r, side in ((3, low, upper), (5, high, lower), (4, low + 1, upper), (6, high + 1, lower)):
        number, _ = number_of(partner(r), brick)
        picked[n - 3] = store_v[number, side]
        sends[n] = give(n, picked.at[n - 3], incoming.at[r, side], r)
    number, _ = number_of(partner(1), brick)
    mate[...] = store_v[number]
    sends[2] = give(2, mate, incoming.at[1], 1)
    number, _ = number_of(brick, brick)
    incoming[0] = store_v[number]

    for load in loads[1:]:
        load.wait()
    tabulate = make_tabulate(rows_ref, cols_ref, phi_v, row_t, col_t)
    lax.fori_loop(0, blocks, tabulate, 0)

    sends[0].wait_recv()
    sends[1].wait_recv()
    relays = (
        (7, low, high, upper), (9, high, low, lower),
        (8, low + 1, high, upper), (10, high + 1, low, lower),
        (11, 1, high, upper), (12, 1, low, lower),
    )
    for n, r, via, side in relays:
        number, _ = number_of(partner(r), partner(via))
        picked[n - 3] = stage[0 if via == high else 1, number]
        sends[n] = give(n, picked.at[n - 3], incoming.at[r ^ via, side], r)
    number, _ = number_of(brick, partner(high))
    incoming[high, upper] = stage[0, number]
    number, _ = number_of(brick, partner(low))
    incoming[low, lower] = stage[1, number]

    arrivals = (
        (0, ()), (1, (2,)), (low, (3,)), (high, (5,)), (low + 1, (4, 12)), (high + 1, (6, 11)),
        (low + high, (7, 9)), (low + high + 1, (8, 10)),
    )
    density = jnp.zeros((1, points), jnp.float32)
    for step, (r, needs) in enumerate(arrivals):
        where, taken = position_in(crossing_ref, own, brick, partner(r) if r else brick)
        for n in needs:
            sends[n].wait_recv()
        product = jnp.dot(incoming[r], col_t[where], preferred_element_type=jnp.float32)
        term = jnp.sum(row_t[where].astype(jnp.float32) * product, axis=0, keepdims=True)
        density = density + jnp.where(taken == 1, term, 0.0)
        if step < len(arrivals) - 1:
            spread(step)
    for n in range(len(arrivals) - 1, groups):
        spread(n)
    for x in range(tall):
        dens[x : x + 1, :] = density[:, x * wide : (x + 1) * wide]
    around = [(dg, db) for dg in (-1, 0, 1) for db in (-1, 0, 1) if (dg, db) != (0, 0)]
    exchange = []
    for n, (dg, db) in enumerate(around):
        target = (lax.rem(group + dg % groups, groups), lax.rem(brick + db % bricks, bricks))
        copy = pltpu.make_async_remote_copy(
            src_ref=dens, dst_ref=halo.at[1 - dg, 1 - db],
            send_sem=halo_send.at[n], recv_sem=halo_recv.at[n],
            device_id=target, device_id_type=MESH,
        )
        copy.start()
        exchange.append(copy)
    halo[1, 1] = dens[...]
    for n in sends:
        sends[n].wait_send()
    for copy in exchange:
        copy.wait()
    scaled = scaled_potential(halo, size_z)

    def partial_of(r):
        where, _ = position_in(crossing_ref, own, brick, partner(r) if r else brick)
        weighted = (col_t[where].astype(jnp.float32) * scaled).astype(jnp.bfloat16)
        return lax.dot_general(row_t[where], weighted, NT, preferred_element_type=jnp.float32)

    give = sender(back_send, back_recv)
    returns = {}
    routes = {
        low + high: ((0, upper, relay.at[0, 1], low), (2, lower, relay.at[1, 1], high)),
        low + high + 1: ((1, upper, relay.at[0, 2], low + 1), (3, lower, relay.at[1, 2], high + 1)),
        high + 1: ((6, lower, direct.at[3], high + 1), (4, upper, relay.at[0, 0], 1)),
        low + 1: ((7, upper, direct.at[1], low + 1), (5, lower, relay.at[1, 0], 1)),
        low: ((8, upper, direct.at[0], low),),
        high: ((9, lower, direct.at[2], high),),
    }
    for r, ways in routes.items():
        value = partial_of(r)
        back[r] = value.astype(jnp.bfloat16)
        if r == low:
            kept[1] = value[half:]
        if r == high:
            kept[0] = value[:half]
        for n, side, target, over in ways:
            returns[n] = give(n, back.at[r, side], target, over)
    back[1] = partial_of(1).astype(jnp.bfloat16)
    returns[10] = give(10, back.at[1], mate_back, 1)
    value = partial_of(0)
    number, taken = number_of(brick, brick)
    for k in range(own):
        out_ref[k] = jnp.where((taken == 1) & (number == k), value, 0.0)

    for n in range(6):
        returns[n].wait_recv()
    first = 11
    for k in range(own):
        for side, via, other in ((0, high, low), (1, low, high)):
            total = jnp.zeros((half, width), jnp.float32)
            for n, r in enumerate((0, 1, other, other + 1)):
                number, taken = number_of(partner(r) if r else brick, partner(via))
                value = relay[side, n - 1].astype(jnp.float32) if n else kept[side]
                total = total + jnp.where((taken == 1) & (number == k), value, 0.0)
            sums[side, k] = total.astype(jnp.bfloat16)
            n = first + 2 * k + side
            returns[n] = give(n, sums.at[side, k], sums_back.at[side, k], via)

    for n in range(6, first):
        returns[n].wait_recv()
    for side, rows, other in ((0, upper, low), (1, lower, high)):
        pieces = []
        for r in (1, other, other + 1):
            number, taken = number_of(partner(r), brick)
            value = mate_back[rows] if r == 1 else direct[2 * side + r - other]
            pieces.append((number, taken, value.astype(jnp.float32)))
        for k in range(own):
            total = out_ref[k, rows]
            for number, taken, value in pieces:
                total = total + jnp.where((taken == 1) & (number == k), value, 0.0)
            out_ref[k, rows] = total
    for k in range(own):
        for side, rows in ((0, upper), (1, lower)):
            returns[first + 2 * k + side].wait_recv()
            out_ref[k, rows] = out_ref[k, rows] + sums_back[side, k].astype(jnp.float32)
    for n in returns:
        returns[n].wait_send()


def cube_call(groups, bricks, store, crossing, phi, rows_index, cols_index):
    own, width = store.shape[0], store.shape[1]
    blocks = crossing.shape[0]
    size_x, size_y, size_z, functions = phi.shape
    points = size_x * size_y * size_z
    tall, wide = size_x, size_y * size_z
    half = width // 2
    hbm = pl.BlockSpec(memory_space=pl.ANY)
    tables = (blocks, width, points)
    back_copies = 11 + 2 * own
    return pl.pallas_call(
        functools.partial(cube_kernel, groups, bricks, size_z),
        out_shape=jax.ShapeDtypeStruct((own, width, width), jnp.float32),
        in_specs=[pl.BlockSpec(memory_space=pltpu.SMEM), hbm, hbm, hbm, hbm],
        out_specs=pl.BlockSpec(memory_space=pltpu.VMEM),
        scratch_shapes=[
            pltpu.VMEM(rows_index.shape, jnp.int32),
            pltpu.VMEM(cols_index.shape, jnp.int32),
            pltpu.VMEM((own, width, width), jnp.bfloat16),
            pltpu.VMEM((points, functions), jnp.bfloat16),
            pltpu.VMEM((width, width), jnp.bfloat16),
            pltpu.VMEM((10, half, width), jnp.bfloat16),
            pltpu.VMEM((2, own, half, width), jnp.bfloat16),
            pltpu.VMEM((bricks, width, width), jnp.bfloat16),
            pltpu.VMEM(tables, jnp.bfloat16),
            pltpu.VMEM(tables, jnp.bfloat16),
            pltpu.VMEM((tall, wide), jnp.float32),
            pltpu.VMEM((3, 3, tall, wide), jnp.float32),
            pltpu.VMEM((bricks, width, width), jnp.bfloat16),
            pltpu.VMEM((2, half, width), jnp.float32),
            pltpu.VMEM((2, 3, half, width), jnp.bfloat16),
            pltpu.VMEM((2, own, half, width), jnp.bfloat16),
            pltpu.VMEM((4, half, width), jnp.bfloat16),
            pltpu.VMEM((width, width), jnp.bfloat16),
            pltpu.VMEM((2, own, half, width), jnp.bfloat16),
            pltpu.SemaphoreType.DMA((4,)),
            pltpu.SemaphoreType.DMA((13,)),
            pltpu.SemaphoreType.DMA((13,)),
            pltpu.SemaphoreType.REGULAR((groups,)),
            pltpu.SemaphoreType.DMA((8,)),
            pltpu.SemaphoreType.DMA((8,)),
            pltpu.SemaphoreType.DMA((back_copies,)),
            pltpu.SemaphoreType.DMA((back_copies,)),
        ],
        compiler_params=pltpu.CompilerParams(
            collective_id=0, has_side_effects=True, vmem_limit_bytes=60 << 20
        ),
    )(crossing, rows_index, cols_index, store, phi.reshape(points, functions))


def local(groups, bricks, store, crossing, phi, rows_index, cols_index):
    own, width = store.shape[0], store.shape[1]
    crossing = crossing.T
    blocks = crossing.shape[0]
    size_x, size_y, size_z, functions = phi.shape
    points = size_x * size_y * size_z
    tall, wide = size_x, size_y * size_z
    slots = (bricks, width, width)
    if bricks == CORE * LOW * HIGH:
        return cube_call(groups, bricks, store, crossing, phi, rows_index, cols_index)
    return pl.pallas_call(
        functools.partial(kernel, groups, bricks, size_z),
        out_shape=jax.ShapeDtypeStruct((own, width, width), jnp.float32),
        in_specs=[
            pl.BlockSpec(memory_space=pltpu.SMEM),
            pl.BlockSpec(memory_space=pl.ANY),
            pl.BlockSpec(memory_space=pl.ANY),
            pl.BlockSpec(memory_space=pl.ANY),
            pl.BlockSpec(memory_space=pl.ANY),
        ],
        out_specs=pl.BlockSpec(memory_space=pltpu.VMEM),
        scratch_shapes=[
            pltpu.VMEM(rows_index.shape, jnp.int32),
            pltpu.VMEM(cols_index.shape, jnp.int32),
            pltpu.VMEM((own, width, width), jnp.bfloat16),
            pltpu.VMEM((points, functions), jnp.bfloat16),
            pltpu.VMEM(slots, jnp.bfloat16),
            pltpu.VMEM(slots, jnp.bfloat16),
            pltpu.VMEM((blocks, width, points), jnp.bfloat16),
            pltpu.VMEM((blocks, width, points), jnp.bfloat16),
            pltpu.VMEM((tall, wide), jnp.float32),
            pltpu.VMEM((3, 3, tall, wide), jnp.float32),
            pltpu.VMEM(slots, jnp.bfloat16),
            pltpu.VMEM(slots, jnp.bfloat16),
            pltpu.SemaphoreType.DMA((4,)),
            pltpu.SemaphoreType.DMA((bricks,)),
            pltpu.SemaphoreType.DMA((bricks,)),
            pltpu.SemaphoreType.DMA((8,)),
            pltpu.SemaphoreType.DMA((8,)),
            pltpu.SemaphoreType.DMA((bricks,)),
            pltpu.SemaphoreType.DMA((bricks,)),
        ],
        compiler_params=pltpu.CompilerParams(
            collective_id=0, has_side_effects=True, vmem_limit_bytes=60 << 20
        ),
    )(crossing, rows_index, cols_index, store, phi.reshape(points, functions))


def solution(mesh):
    in_specs = (
        P(("grp", "brick"), None, None),
        P("grp", None),
        P("grp", "brick", None, None),
        P(("grp", "brick"), None, None),
        P(("grp", "brick"), None, None),
    )
    out_specs = P(("grp", "brick"), None, None)
    body = functools.partial(local, mesh.shape["grp"], mesh.shape["brick"])
    return jax.shard_map(body, mesh=mesh, in_specs=in_specs, out_specs=out_specs, check_vma=False)
```

```python
import functools
import math

import jax
import jax.numpy as jnp
from jax import lax
from jax.experimental import pallas as pl
from jax.experimental.pallas import tpu as pltpu
from jax.sharding import PartitionSpec as P

GRAD_WEIGHT = 0.5
CORE, LOW, HIGH = 2, 2, 2
MESH = pl.DeviceIdType.MESH
NT = (((1,), (1,)), ((), ()))


def partner_of(bricks, brick, r):
    if bricks & (bricks - 1):
        return lax.rem(r - brick + bricks, bricks)
    other = brick
    for bit in range(bricks.bit_length() - 1):
        if r >> bit & 1:
            other = other + (1 << bit) * (1 - 2 * lax.rem(lax.div(brick, 1 << bit), 2))
    return other


def block_number(crossing_ref, own, whom, owner):
    number, taken = jnp.int32(0), jnp.int32(0)
    for j in range(crossing_ref.shape[0]):
        entry = crossing_ref[j, whom]
        hit = lax.div(entry, own) == owner
        number = jnp.where(hit, lax.rem(entry, own), number)
        taken = jnp.where(hit, 1, taken)
    return number, taken


def make_tabulate(rows_ref, cols_ref, phi_v, row_t, col_t):
    width, functions = row_t.shape[1], phi_v.shape[1]
    lane = lax.broadcasted_iota(jnp.int32, (width, 128), 1)

    def pick(index_ref, table_ref, j):
        index = jnp.broadcast_to(index_ref[0, pl.ds(j, 1), :], (128, width)).T
        onehot = jnp.concatenate(
            [
                jnp.where(index == lane + k * 128, 1.0, 0.0).astype(jnp.bfloat16)
                for k in range(functions // 128)
            ],
            axis=1,
        )
        table_ref[j] = lax.dot_general(
            onehot, phi_v[...], NT, preferred_element_type=jnp.float32
        ).astype(jnp.bfloat16)

    def tabulate(j, carry):
        pick(rows_ref, row_t, j)
        pick(cols_ref, col_t, j)
        return carry

    return tabulate


def scaled_potential(halo, size_z):
    tall, wide = halo.shape[2:]
    points = tall * wide
    field = jnp.concatenate(
        [jnp.concatenate([halo[i, k] for k in range(3)], axis=1) for i in range(3)], axis=0
    )
    rows, lanes = field.shape
    depth = lax.rem(lax.broadcasted_iota(jnp.int32, field.shape, 1), size_z)

    def along_x(f):
        return (pltpu.roll(f, rows - 1, 0) - pltpu.roll(f, 1, 0)) * 0.5

    def along_y(f):
        return (pltpu.roll(f, lanes - size_z, 1) - pltpu.roll(f, size_z, 1)) * 0.5

    def along_z(f):
        up = jnp.where(
            depth == size_z - 1, pltpu.roll(f, size_z - 1, 1), pltpu.roll(f, lanes - 1, 1)
        )
        down = jnp.where(depth == 0, pltpu.roll(f, lanes - size_z + 1, 1), pltpu.roll(f, 1, 1))
        return (up - down) * 0.5

    grad_x, grad_y, grad_z = along_x(field), along_y(field), along_z(field)
    sigma = grad_x * grad_x + grad_y * grad_y + grad_z * grad_z
    factor = 2.0 * GRAD_WEIGHT / (1.0 + sigma)
    diverge = along_x(factor * grad_x) + along_y(factor * grad_y) + along_z(factor * grad_z)
    centre = field[tall : 2 * tall, wide : 2 * wide]
    potential = centre / jnp.sqrt(1.0 + centre * centre) - diverge[
        tall : 2 * tall, wide : 2 * wide
    ]
    scaled = potential * (1.0 / math.sqrt(points))
    scaled = jnp.concatenate([scaled[x : x + 1, :] for x in range(tall)], axis=1)
    return scaled


def position_in(crossing_ref, own, whom, owner):
    where, taken = jnp.int32(0), jnp.int32(0)
    for j in range(crossing_ref.shape[0]):
        hit = lax.div(crossing_ref[j, whom], own) == owner
        where = jnp.where(hit, j, where)
        taken = jnp.where(hit, 1, taken)
    return where, taken


def kernel(
    groups, bricks, size_z,
    crossing_ref, rows_hbm, cols_hbm, store_hbm, phi_hbm, out_ref,
    rows_ref, cols_ref, store_v, phi_v, outgoing, incoming, row_t, col_t, dens, halo, back, landed,
    load_sem, send_sem, recv_sem, halo_send, halo_recv, back_send, back_recv,
):
    group = lax.axis_index("grp")
    brick = lax.axis_index("brick")
    own, width = store_v.shape[0], store_v.shape[1]
    blocks = crossing_ref.shape[0]
    points, functions = phi_v.shape
    tall, wide = dens.shape

    load_store = pltpu.make_async_copy(store_hbm, store_v, load_sem.at[0])
    load_phi = pltpu.make_async_copy(phi_hbm, phi_v, load_sem.at[1])
    load_rows = pltpu.make_async_copy(rows_hbm, rows_ref, load_sem.at[2])
    load_cols = pltpu.make_async_copy(cols_hbm, cols_ref, load_sem.at[3])
    load_store.start()
    load_phi.start()
    load_rows.start()
    load_cols.start()

    def member(offset):
        return lax.rem(brick + (offset % bricks), bricks)

    partner = functools.partial(partner_of, bricks, brick)
    order = sorted(range(1, bricks), key=lambda r: (r == 1, r & 1, bin(r >> 1).count("1")))

    def place(dg, db):
        return (lax.rem(group + (dg % groups), groups), member(db))

    around = [(dg, db) for dg in (-1, 0, 1) for db in (-1, 0, 1) if (dg, db) != (0, 0)]
    reached = {(0, r) for r in range(1, bricks)}
    reached |= {(dg % groups, db % bricks) for dg, db in around}
    reached = sorted(reached)
    barrier = pltpu.get_barrier_semaphore()
    for dg, db in reached:
        pl.semaphore_signal(barrier, inc=1, device_id=place(dg, db), device_id_type=MESH)

    position_of = functools.partial(position_in, crossing_ref, own, brick)

    load_store.wait()
    for r in order:
        number, _ = block_number(crossing_ref, own, partner(r), brick)
        outgoing[r] = store_v[number]
    number, _ = block_number(crossing_ref, own, brick, brick)
    incoming[0] = store_v[number]
    pl.semaphore_wait(barrier, len(reached))
    sends = []
    for r in order:
        copy = pltpu.make_async_remote_copy(
            src_ref=outgoing.at[r], dst_ref=incoming.at[r],
            send_sem=send_sem.at[r], recv_sem=recv_sem.at[r],
            device_id=(group, partner(r)), device_id_type=MESH,
        )
        copy.start()
        sends.append(copy)

    load_rows.wait()
    load_cols.wait()
    load_phi.wait()
    tabulate = make_tabulate(rows_ref, cols_ref, phi_v, row_t, col_t)
    lax.fori_loop(0, blocks, tabulate, 0)

    density = jnp.zeros((1, points), jnp.float32)
    for n, r in enumerate([0] + order):
        where, taken = position_of(partner(r) if r else brick)
        if n:
            sends[n - 1].wait()
        product = jnp.dot(incoming[r], col_t[where], preferred_element_type=jnp.float32)
        term = jnp.sum(row_t[where].astype(jnp.float32) * product, axis=0, keepdims=True)
        density = density + jnp.where(taken == 1, term, 0.0)
    for x in range(tall):
        dens[x : x + 1, :] = density[:, x * wide : (x + 1) * wide]
    halo[1, 1] = dens[...]
    exchange = []
    for n, (dg, db) in enumerate(around):
        copy = pltpu.make_async_remote_copy(
            src_ref=dens, dst_ref=halo.at[1 - dg, 1 - db],
            send_sem=halo_send.at[n], recv_sem=halo_recv.at[n],
            device_id=place(dg, db), device_id_type=MESH,
        )
        copy.start()
        exchange.append(copy)
    for copy in exchange:
        copy.wait()

    scaled = scaled_potential(halo, size_z)

    returns = []
    for r in order + [0]:
        where, _ = position_of(partner(r) if r else brick)
        weighted = (col_t[where].astype(jnp.float32) * scaled).astype(jnp.bfloat16)
        back[r] = lax.dot_general(
            row_t[where], weighted, NT, preferred_element_type=jnp.float32
        ).astype(jnp.bfloat16)
        if r:
            copy = pltpu.make_async_remote_copy(
                src_ref=back.at[r], dst_ref=landed.at[r],
                send_sem=back_send.at[r], recv_sem=back_recv.at[r],
                device_id=(group, partner(r)), device_id_type=MESH,
            )
            copy.start()
            returns.append(copy)
    for n, r in enumerate([0] + order):
        number, taken = block_number(crossing_ref, own, partner(r) if r else brick, brick)
        if n:
            returns[n - 1].wait()
        value = (landed if n else back)[r].astype(jnp.float32)
        for k in range(own):
            term = jnp.where((taken == 1) & (number == k), value, 0.0)
            out_ref[k] = out_ref[k] + term if n else term


def cube_kernel(
    groups, bricks, size_z,
    crossing_ref, rows_hbm, cols_hbm, store_hbm, phi_hbm, near_hbm, far_hbm,
    rows_ref, cols_ref, store_v, phi_v, mate, picked, stage, incoming, row_t, col_t,
    dens, halo, back, kept, relay, sums, direct, mate_back, total_v,
    load_sem, near_sem, send_sem, recv_sem, ready, halo_send, halo_recv, back_send, back_recv,
):
    group = lax.axis_index("grp")
    brick = lax.axis_index("brick")
    own, width = store_v.shape[0], store_v.shape[1]
    half = width // 2
    points = phi_v.shape[0]
    blocks = crossing_ref.shape[0]
    tall, wide = dens.shape
    upper, lower = pl.ds(0, half), pl.ds(half, half)
    low, high = CORE, CORE * LOW
    partner = functools.partial(partner_of, bricks, brick)
    number_of = functools.partial(block_number, crossing_ref, own)

    loads = [
        pltpu.make_async_copy(source, target, load_sem.at[n])
        for n, (source, target) in enumerate(
            ((store_hbm, store_v), (rows_hbm, rows_ref), (cols_hbm, cols_ref), (phi_hbm, phi_v))
        )
    ]
    barrier = pltpu.get_barrier_semaphore()
    near = (1, low, low + 1, high, high + 1)

    def along_chain(semaphore):
        @pl.when(group > 0)
        def _():
            pl.semaphore_signal(
                semaphore, inc=1, device_id=(group - 1, brick), device_id_type=MESH
            )

        @pl.when(group < groups - 1)
        def _():
            pl.semaphore_signal(
                semaphore, inc=1, device_id=(group + 1, brick), device_id_type=MESH
            )

    links = jnp.where(group > 0, 1, 0) + jnp.where(group < groups - 1, 1, 0)
    for r in near:
        pl.semaphore_signal(barrier, inc=1, device_id=(group, partner(r)), device_id_type=MESH)
    along_chain(barrier)
    for load in loads:
        load.start()
    pl.semaphore_wait(barrier, len(near) + links)

    for r in near:
        pl.semaphore_signal(ready.at[0], inc=1, device_id=(group, partner(r)), device_id_type=MESH)

    def spread(n):
        if n >= groups:
            return
        pl.semaphore_wait(ready.at[n], links if n else len(near))
        if n + 1 < groups:
            along_chain(ready.at[n + 1])

    def sender(send, recv):
        def start(n, source, target, r):
            copy = pltpu.make_async_remote_copy(
                src_ref=source, dst_ref=target, send_sem=send.at[n], recv_sem=recv.at[n],
                device_id=(group, partner(r)), device_id_type=MESH,
            )
            copy.start()
            return copy
        return start

    give = sender(send_sem, recv_sem)
    sends = {}
    sends[0] = give(0, store_hbm.at[:, upper], stage.at[0], high)
    sends[1] = give(1, store_hbm.at[:, lower], stage.at[1], low)
    loads[0].wait()
    for n, r, side in ((3, low, upper), (5, high, lower), (4, low + 1, upper), (6, high + 1, lower)):
        number, _ = number_of(partner(r), brick)
        picked[n - 3] = store_v[number, side]
        sends[n] = give(n, picked.at[n - 3], incoming.at[r, side], r)
    number, _ = number_of(partner(1), brick)
    mate[...] = store_v[number]
    sends[2] = give(2, mate, incoming.at[1], 1)
    number, _ = number_of(brick, brick)
    incoming[0] = store_v[number]

    for load in loads[1:]:
        load.wait()
    tabulate = make_tabulate(rows_ref, cols_ref, phi_v, row_t, col_t)
    lax.fori_loop(0, blocks // 2, tabulate, 0)
    spread(0)
    lax.fori_loop(blocks // 2, blocks, tabulate, 0)
    spread(1)

    sends[0].wait_recv()
    sends[1].wait_recv()
    relays = (
        (11, 1, high, upper), (12, 1, low, lower),
        (7, low, high, upper), (9, high, low, lower),
        (8, low + 1, high, upper), (10, high + 1, low, lower),
    )
    for n, r, via, side in relays:
        number, _ = number_of(partner(r), partner(via))
        picked[n - 3] = stage[0 if via == high else 1, number]
        sends[n] = give(n, picked.at[n - 3], incoming.at[r ^ via, side], r)
    number, _ = number_of(brick, partner(high))
    incoming[high, upper] = stage[0, number]
    number, _ = number_of(brick, partner(low))
    incoming[low, lower] = stage[1, number]

    arrivals = (
        (0, ()), (1, (2,)), (low, (3,)), (high, (5,)), (low + 1, (4, 12)), (high + 1, (6, 11)),
        (low + high, (7, 9)), (low + high + 1, (8, 10)),
    )
    density = jnp.zeros((1, points), jnp.float32)
    for step, (r, needs) in enumerate(arrivals):
        where, taken = position_in(crossing_ref, own, brick, partner(r) if r else brick)
        for n in needs:
            sends[n].wait_recv()
        product = jnp.dot(incoming[r], col_t[where], preferred_element_type=jnp.float32)
        term = jnp.sum(row_t[where].astype(jnp.float32) * product, axis=0, keepdims=True)
        density = density + jnp.where(taken == 1, term, 0.0)
        if step < len(arrivals) - 1:
            spread(step + 2)
    for n in range(len(arrivals) + 1, groups):
        spread(n)
    for x in range(tall):
        dens[x : x + 1, :] = density[:, x * wide : (x + 1) * wide]
    around = [(dg, db) for dg in (-1, 0, 1) for db in (-1, 0, 1) if (dg, db) != (0, 0)]
    exchange = []
    for n, (dg, db) in enumerate(around):
        target = (lax.rem(group + dg % groups, groups), lax.rem(brick + db % bricks, bricks))
        copy = pltpu.make_async_remote_copy(
            src_ref=dens, dst_ref=halo.at[1 - dg, 1 - db],
            send_sem=halo_send.at[n], recv_sem=halo_recv.at[n],
            device_id=target, device_id_type=MESH,
        )
        copy.start()
        exchange.append(copy)
    halo[1, 1] = dens[...]
    for n in sends:
        sends[n].wait_send()
    for copy in exchange:
        copy.wait()
    scaled = scaled_potential(halo, size_z)

    def partial_of(r):
        where, _ = position_in(crossing_ref, own, brick, partner(r) if r else brick)
        weighted = (col_t[where].astype(jnp.float32) * scaled).astype(jnp.bfloat16)
        return lax.dot_general(row_t[where], weighted, NT, preferred_element_type=jnp.float32)

    give = sender(back_send, back_recv)
    returns = {}
    routes = {
        low + high: ((0, upper, relay.at[0, 1], low), (2, lower, relay.at[1, 1], high)),
        low + high + 1: ((1, upper, relay.at[0, 2], low + 1), (3, lower, relay.at[1, 2], high + 1)),
        high + 1: ((6, lower, direct.at[3], high + 1), (4, upper, relay.at[0, 0], 1)),
        low + 1: ((7, upper, direct.at[1], low + 1), (5, lower, relay.at[1, 0], 1)),
        low: ((8, upper, direct.at[0], low),),
        high: ((9, lower, direct.at[2], high),),
    }
    for r, ways in routes.items():
        value = partial_of(r)
        back[r] = value.astype(jnp.bfloat16)
        if r == low:
            kept[1] = value[half:]
        if r == high:
            kept[0] = value[:half]
        for n, side, target, over in ways:
            returns[n] = give(n, back.at[r, side], target, over)
    back[1] = partial_of(1).astype(jnp.bfloat16)
    returns[10] = give(10, back.at[1], mate_back, 1)
    value = partial_of(0)
    number, taken = number_of(brick, brick)
    for k in range(own):
        total_v[k] = jnp.where((taken == 1) & (number == k), value, 0.0)

    for n in range(6):
        returns[n].wait_recv()
    first = 11
    for k in range(own):
        for side, via, other in ((0, high, low), (1, low, high)):
            total = jnp.zeros((half, width), jnp.float32)
            for n, r in enumerate((0, 1, other, other + 1)):
                number, taken = number_of(partner(r) if r else brick, partner(via))
                value = relay[side, n - 1].astype(jnp.float32) if n else kept[side]
                total = total + jnp.where((taken == 1) & (number == k), value, 0.0)
            sums[side, k] = total.astype(jnp.bfloat16)
            n = first + 2 * k + side
            returns[n] = give(n, sums.at[side, k], far_hbm.at[k, upper if side == 0 else lower], via)

    for n in range(6, first):
        returns[n].wait_recv()
    for side, rows, other in ((0, upper, low), (1, lower, high)):
        pieces = []
        for r in (1, other, other + 1):
            number, taken = number_of(partner(r), brick)
            value = mate_back[rows] if r == 1 else direct[2 * side + r - other]
            pieces.append((number, taken, value.astype(jnp.float32)))
        for k in range(own):
            total = total_v[k, rows]
            for number, taken, value in pieces:
                total = total + jnp.where((taken == 1) & (number == k), value, 0.0)
            total_v[k, rows] = total
    keep = pltpu.make_async_copy(total_v, near_hbm, near_sem)
    keep.start()
    keep.wait()
    for n in range(first, first + 2 * own):
        returns[n].wait_recv()
    for n in returns:
        returns[n].wait_send()


def cube_call(groups, bricks, store, crossing, phi, rows_index, cols_index):
    own, width = store.shape[0], store.shape[1]
    blocks = crossing.shape[0]
    size_x, size_y, size_z, functions = phi.shape
    points = size_x * size_y * size_z
    tall, wide = size_x, size_y * size_z
    half = width // 2
    hbm = pl.BlockSpec(memory_space=pl.ANY)
    tables = (blocks, width, points)
    back_copies = 11 + 2 * own
    near, far = pl.pallas_call(
        functools.partial(cube_kernel, groups, bricks, size_z),
        out_shape=[
            jax.ShapeDtypeStruct((own, width, width), jnp.float32),
            jax.ShapeDtypeStruct((own, width, width), jnp.bfloat16),
        ],
        in_specs=[pl.BlockSpec(memory_space=pltpu.SMEM), hbm, hbm, hbm, hbm],
        out_specs=[hbm, hbm],
        scratch_shapes=[
            pltpu.VMEM(rows_index.shape, jnp.int32),
            pltpu.VMEM(cols_index.shape, jnp.int32),
            pltpu.VMEM((own, width, width), jnp.bfloat16),
            pltpu.VMEM((points, functions), jnp.bfloat16),
            pltpu.VMEM((width, width), jnp.bfloat16),
            pltpu.VMEM((10, half, width), jnp.bfloat16),
            pltpu.VMEM((2, own, half, width), jnp.bfloat16),
            pltpu.VMEM((bricks, width, width), jnp.bfloat16),
            pltpu.VMEM(tables, jnp.bfloat16),
            pltpu.VMEM(tables, jnp.bfloat16),
            pltpu.VMEM((tall, wide), jnp.float32),
            pltpu.VMEM((3, 3, tall, wide), jnp.float32),
            pltpu.VMEM((bricks, width, width), jnp.bfloat16),
            pltpu.VMEM((2, half, width), jnp.float32),
            pltpu.VMEM((2, 3, half, width), jnp.bfloat16),
            pltpu.VMEM((2, own, half, width), jnp.bfloat16),
            pltpu.VMEM((4, half, width), jnp.bfloat16),
            pltpu.VMEM((width, width), jnp.bfloat16),
            pltpu.VMEM((own, width, width), jnp.float32),
            pltpu.SemaphoreType.DMA((4,)),
            pltpu.SemaphoreType.DMA,
            pltpu.SemaphoreType.DMA((13,)),
            pltpu.SemaphoreType.DMA((13,)),
            pltpu.SemaphoreType.REGULAR((groups,)),
            pltpu.SemaphoreType.DMA((8,)),
            pltpu.SemaphoreType.DMA((8,)),
            pltpu.SemaphoreType.DMA((back_copies,)),
            pltpu.SemaphoreType.DMA((back_copies,)),
        ],
        compiler_params=pltpu.CompilerParams(
            collective_id=0, has_side_effects=True, vmem_limit_bytes=60 << 20
        ),
    )(crossing, rows_index, cols_index, store, phi.reshape(points, functions))
    return near + far.astype(jnp.float32)


def local(groups, bricks, store, crossing, phi, rows_index, cols_index):
    own, width = store.shape[0], store.shape[1]
    crossing = crossing.T
    blocks = crossing.shape[0]
    size_x, size_y, size_z, functions = phi.shape
    points = size_x * size_y * size_z
    tall, wide = size_x, size_y * size_z
    slots = (bricks, width, width)
    if bricks == CORE * LOW * HIGH:
        return cube_call(groups, bricks, store, crossing, phi, rows_index, cols_index)
    return pl.pallas_call(
        functools.partial(kernel, groups, bricks, size_z),
        out_shape=jax.ShapeDtypeStruct((own, width, width), jnp.float32),
        in_specs=[
            pl.BlockSpec(memory_space=pltpu.SMEM),
            pl.BlockSpec(memory_space=pl.ANY),
            pl.BlockSpec(memory_space=pl.ANY),
            pl.BlockSpec(memory_space=pl.ANY),
            pl.BlockSpec(memory_space=pl.ANY),
        ],
        out_specs=pl.BlockSpec(memory_space=pltpu.VMEM),
        scratch_shapes=[
            pltpu.VMEM(rows_index.shape, jnp.int32),
            pltpu.VMEM(cols_index.shape, jnp.int32),
            pltpu.VMEM((own, width, width), jnp.bfloat16),
            pltpu.VMEM((points, functions), jnp.bfloat16),
            pltpu.VMEM(slots, jnp.bfloat16),
            pltpu.VMEM(slots, jnp.bfloat16),
            pltpu.VMEM((blocks, width, points), jnp.bfloat16),
            pltpu.VMEM((blocks, width, points), jnp.bfloat16),
            pltpu.VMEM((tall, wide), jnp.float32),
            pltpu.VMEM((3, 3, tall, wide), jnp.float32),
            pltpu.VMEM(slots, jnp.bfloat16),
            pltpu.VMEM(slots, jnp.bfloat16),
            pltpu.SemaphoreType.DMA((4,)),
            pltpu.SemaphoreType.DMA((bricks,)),
            pltpu.SemaphoreType.DMA((bricks,)),
            pltpu.SemaphoreType.DMA((8,)),
            pltpu.SemaphoreType.DMA((8,)),
            pltpu.SemaphoreType.DMA((bricks,)),
            pltpu.SemaphoreType.DMA((bricks,)),
        ],
        compiler_params=pltpu.CompilerParams(
            collective_id=0, has_side_effects=True, vmem_limit_bytes=60 << 20
        ),
    )(crossing, rows_index, cols_index, store, phi.reshape(points, functions))


def solution(mesh):
    in_specs = (
        P(("grp", "brick"), None, None),
        P("grp", None),
        P("grp", "brick", None, None),
        P(("grp", "brick"), None, None),
        P(("grp", "brick"), None, None),
    )
    out_specs = P(("grp", "brick"), None, None)
    body = functools.partial(local, mesh.shape["grp"], mesh.shape["brick"])
    return jax.shard_map(body, mesh=mesh, in_specs=in_specs, out_specs=out_specs, check_vma=False)
```

```python
import functools
import math

import jax
import jax.numpy as jnp
from jax import lax
from jax.experimental import pallas as pl
from jax.experimental.pallas import tpu as pltpu
from jax.sharding import PartitionSpec as P

GRAD_WEIGHT = 0.5
CORE, LOW, HIGH = 2, 2, 2
MESH = pl.DeviceIdType.MESH
NT = (((1,), (1,)), ((), ()))


def partner_of(bricks, brick, r):
    if bricks & (bricks - 1):
        return lax.rem(r - brick + bricks, bricks)
    other = brick
    for bit in range(bricks.bit_length() - 1):
        if r >> bit & 1:
            other = other + (1 << bit) * (1 - 2 * lax.rem(lax.div(brick, 1 << bit), 2))
    return other


def block_number(crossing_ref, own, whom, owner):
    number, taken = jnp.int32(0), jnp.int32(0)
    for j in range(crossing_ref.shape[0]):
        entry = crossing_ref[j, whom]
        hit = lax.div(entry, own) == owner
        number = jnp.where(hit, lax.rem(entry, own), number)
        taken = jnp.where(hit, 1, taken)
    return number, taken


def make_tabulate(rows_ref, cols_ref, phi_v, row_t, col_t):
    width, functions = row_t.shape[1], phi_v.shape[1]
    lane = lax.broadcasted_iota(jnp.int32, (width, 128), 1)

    def pick(index_ref, table_ref, j):
        index = jnp.broadcast_to(index_ref[0, pl.ds(j, 1), :], (128, width)).T
        onehot = jnp.concatenate(
            [
                jnp.where(index == lane + k * 128, 1.0, 0.0).astype(jnp.bfloat16)
                for k in range(functions // 128)
            ],
            axis=1,
        )
        table_ref[j] = lax.dot_general(
            onehot, phi_v[...], NT, preferred_element_type=jnp.float32
        ).astype(jnp.bfloat16)

    def tabulate(j, carry):
        pick(rows_ref, row_t, j)
        pick(cols_ref, col_t, j)
        return carry

    return tabulate


def scaled_potential(halo, size_z):
    tall, wide = halo.shape[2:]
    points = tall * wide
    field = jnp.concatenate(
        [jnp.concatenate([halo[i, k] for k in range(3)], axis=1) for i in range(3)], axis=0
    )
    rows, lanes = field.shape
    depth = lax.rem(lax.broadcasted_iota(jnp.int32, field.shape, 1), size_z)

    def along_x(f):
        return (pltpu.roll(f, rows - 1, 0) - pltpu.roll(f, 1, 0)) * 0.5

    def along_y(f):
        return (pltpu.roll(f, lanes - size_z, 1) - pltpu.roll(f, size_z, 1)) * 0.5

    def along_z(f):
        up = jnp.where(
            depth == size_z - 1, pltpu.roll(f, size_z - 1, 1), pltpu.roll(f, lanes - 1, 1)
        )
        down = jnp.where(depth == 0, pltpu.roll(f, lanes - size_z + 1, 1), pltpu.roll(f, 1, 1))
        return (up - down) * 0.5

    grad_x, grad_y, grad_z = along_x(field), along_y(field), along_z(field)
    sigma = grad_x * grad_x + grad_y * grad_y + grad_z * grad_z
    factor = 2.0 * GRAD_WEIGHT / (1.0 + sigma)
    diverge = along_x(factor * grad_x) + along_y(factor * grad_y) + along_z(factor * grad_z)
    centre = field[tall : 2 * tall, wide : 2 * wide]
    potential = centre / jnp.sqrt(1.0 + centre * centre) - diverge[
        tall : 2 * tall, wide : 2 * wide
    ]
    scaled = potential * (1.0 / math.sqrt(points))
    scaled = jnp.concatenate([scaled[x : x + 1, :] for x in range(tall)], axis=1)
    return scaled


def position_in(crossing_ref, own, whom, owner):
    where, taken = jnp.int32(0), jnp.int32(0)
    for j in range(crossing_ref.shape[0]):
        hit = lax.div(crossing_ref[j, whom], own) == owner
        where = jnp.where(hit, j, where)
        taken = jnp.where(hit, 1, taken)
    return where, taken


def kernel(
    groups, bricks, size_z,
    crossing_ref, rows_hbm, cols_hbm, store_hbm, phi_hbm, out_ref,
    rows_ref, cols_ref, store_v, phi_v, outgoing, incoming, row_t, col_t, dens, halo, back, landed,
    load_sem, send_sem, recv_sem, halo_send, halo_recv, back_send, back_recv,
):
    group = lax.axis_index("grp")
    brick = lax.axis_index("brick")
    own, width = store_v.shape[0], store_v.shape[1]
    blocks = crossing_ref.shape[0]
    points, functions = phi_v.shape
    tall, wide = dens.shape

    load_store = pltpu.make_async_copy(store_hbm, store_v, load_sem.at[0])
    load_phi = pltpu.make_async_copy(phi_hbm, phi_v, load_sem.at[1])
    load_rows = pltpu.make_async_copy(rows_hbm, rows_ref, load_sem.at[2])
    load_cols = pltpu.make_async_copy(cols_hbm, cols_ref, load_sem.at[3])
    load_store.start()
    load_phi.start()
    load_rows.start()
    load_cols.start()

    def member(offset):
        return lax.rem(brick + (offset % bricks), bricks)

    partner = functools.partial(partner_of, bricks, brick)
    order = sorted(range(1, bricks), key=lambda r: (r == 1, r & 1, bin(r >> 1).count("1")))

    def place(dg, db):
        return (lax.rem(group + (dg % groups), groups), member(db))

    around = [(dg, db) for dg in (-1, 0, 1) for db in (-1, 0, 1) if (dg, db) != (0, 0)]
    reached = {(0, r) for r in range(1, bricks)}
    reached |= {(dg % groups, db % bricks) for dg, db in around}
    reached = sorted(reached)
    barrier = pltpu.get_barrier_semaphore()
    for dg, db in reached:
        pl.semaphore_signal(barrier, inc=1, device_id=place(dg, db), device_id_type=MESH)

    position_of = functools.partial(position_in, crossing_ref, own, brick)

    load_store.wait()
    for r in order:
        number, _ = block_number(crossing_ref, own, partner(r), brick)
        outgoing[r] = store_v[number]
    number, _ = block_number(crossing_ref, own, brick, brick)
    incoming[0] = store_v[number]
    pl.semaphore_wait(barrier, len(reached))
    sends = []
    for r in order:
        copy = pltpu.make_async_remote_copy(
            src_ref=outgoing.at[r], dst_ref=incoming.at[r],
            send_sem=send_sem.at[r], recv_sem=recv_sem.at[r],
            device_id=(group, partner(r)), device_id_type=MESH,
        )
        copy.start()
        sends.append(copy)

    load_rows.wait()
    load_cols.wait()
    load_phi.wait()
    tabulate = make_tabulate(rows_ref, cols_ref, phi_v, row_t, col_t)
    lax.fori_loop(0, blocks, tabulate, 0)

    density = jnp.zeros((1, points), jnp.float32)
    for n, r in enumerate([0] + order):
        where, taken = position_of(partner(r) if r else brick)
        if n:
            sends[n - 1].wait()
        product = jnp.dot(incoming[r], col_t[where], preferred_element_type=jnp.float32)
        term = jnp.sum(row_t[where].astype(jnp.float32) * product, axis=0, keepdims=True)
        density = density + jnp.where(taken == 1, term, 0.0)
    for x in range(tall):
        dens[x : x + 1, :] = density[:, x * wide : (x + 1) * wide]
    halo[1, 1] = dens[...]
    exchange = []
    for n, (dg, db) in enumerate(around):
        copy = pltpu.make_async_remote_copy(
            src_ref=dens, dst_ref=halo.at[1 - dg, 1 - db],
            send_sem=halo_send.at[n], recv_sem=halo_recv.at[n],
            device_id=place(dg, db), device_id_type=MESH,
        )
        copy.start()
        exchange.append(copy)
    for copy in exchange:
        copy.wait()

    scaled = scaled_potential(halo, size_z)

    returns = []
    for r in order + [0]:
        where, _ = position_of(partner(r) if r else brick)
        weighted = (col_t[where].astype(jnp.float32) * scaled).astype(jnp.bfloat16)
        back[r] = lax.dot_general(
            row_t[where], weighted, NT, preferred_element_type=jnp.float32
        ).astype(jnp.bfloat16)
        if r:
            copy = pltpu.make_async_remote_copy(
                src_ref=back.at[r], dst_ref=landed.at[r],
                send_sem=back_send.at[r], recv_sem=back_recv.at[r],
                device_id=(group, partner(r)), device_id_type=MESH,
            )
            copy.start()
            returns.append(copy)
    for n, r in enumerate([0] + order):
        number, taken = block_number(crossing_ref, own, partner(r) if r else brick, brick)
        if n:
            returns[n - 1].wait()
        value = (landed if n else back)[r].astype(jnp.float32)
        for k in range(own):
            term = jnp.where((taken == 1) & (number == k), value, 0.0)
            out_ref[k] = out_ref[k] + term if n else term


def cube_kernel(
    groups, bricks, size_z,
    crossing_ref, rows_hbm, cols_hbm, store_hbm, phi_hbm, near_hbm, far_hbm,
    rows_ref, cols_ref, store_v, phi_v, mate, picked, stage, incoming, row_t, col_t,
    dens, halo, back, kept, relay, sums, direct, mate_back, total_v,
    load_sem, near_sem, send_sem, recv_sem, ready, halo_send, halo_recv, back_send, back_recv,
):
    group = lax.axis_index("grp")
    brick = lax.axis_index("brick")
    own, width = store_v.shape[0], store_v.shape[1]
    half = width // 2
    points = phi_v.shape[0]
    blocks = crossing_ref.shape[0]
    tall, wide = dens.shape
    upper, lower = pl.ds(0, half), pl.ds(half, half)
    low, high = CORE, CORE * LOW
    partner = functools.partial(partner_of, bricks, brick)
    number_of = functools.partial(block_number, crossing_ref, own)

    loads = [
        pltpu.make_async_copy(source, target, load_sem.at[n])
        for n, (source, target) in enumerate(
            ((store_hbm, store_v), (rows_hbm, rows_ref), (cols_hbm, cols_ref), (phi_hbm, phi_v))
        )
    ]
    barrier = pltpu.get_barrier_semaphore()
    near = (1, low, low + 1, high, high + 1)

    def along_chain(semaphore):
        @pl.when(group > 0)
        def _():
            pl.semaphore_signal(
                semaphore, inc=1, device_id=(group - 1, brick), device_id_type=MESH
            )

        @pl.when(group < groups - 1)
        def _():
            pl.semaphore_signal(
                semaphore, inc=1, device_id=(group + 1, brick), device_id_type=MESH
            )

    links = jnp.where(group > 0, 1, 0) + jnp.where(group < groups - 1, 1, 0)
    for r in near:
        pl.semaphore_signal(barrier, inc=1, device_id=(group, partner(r)), device_id_type=MESH)
    along_chain(barrier)
    for load in loads:
        load.start()
    loads[0].wait()
    pl.semaphore_wait(barrier, len(near) + links)

    for r in near:
        pl.semaphore_signal(ready.at[0], inc=1, device_id=(group, partner(r)), device_id_type=MESH)

    def spread(n):
        if n >= groups:
            return
        pl.semaphore_wait(ready.at[n], links if n else len(near))
        if n + 1 < groups:
            along_chain(ready.at[n + 1])

    def sender(send, recv):
        def start(n, source, target, r):
            copy = pltpu.make_async_remote_copy(
                src_ref=source, dst_ref=target, send_sem=send.at[n], recv_sem=recv.at[n],
                device_id=(group, partner(r)), device_id_type=MESH,
            )
            copy.start()
            return copy
        return start

    give = sender(send_sem, recv_sem)
    sends = {}
    sends[0] = give(0, store_v.at[:, upper], stage.at[0], high)
    sends[1] = give(1, store_v.at[:, lower], stage.at[1], low)
    for n, r, side in ((3, low, upper), (5, high, lower), (4, low + 1, upper), (6, high + 1, lower)):
        number, _ = number_of(partner(r), brick)
        picked[n - 3] = store_v[number, side]
        sends[n] = give(n, picked.at[n - 3], incoming.at[r, side], r)
    number, _ = number_of(partner(1), brick)
    mate[...] = store_v[number]
    sends[2] = give(2, mate, incoming.at[1], 1)
    number, _ = number_of(brick, brick)
    incoming[0] = store_v[number]

    for load in loads[1:]:
        load.wait()
    tabulate = make_tabulate(rows_ref, cols_ref, phi_v, row_t, col_t)
    lax.fori_loop(0, blocks // 2, tabulate, 0)
    spread(0)
    lax.fori_loop(blocks // 2, blocks, tabulate, 0)
    spread(1)

    sends[0].wait_recv()
    sends[1].wait_recv()
    relays = (
        (11, 1, high, upper), (12, 1, low, lower),
        (7, low, high, upper), (9, high, low, lower),
        (8, low + 1, high, upper), (10, high + 1, low, lower),
    )
    for n, r, via, side in relays:
        number, _ = number_of(partner(r), partner(via))
        picked[n - 3] = stage[0 if via == high else 1, number]
        sends[n] = give(n, picked.at[n - 3], incoming.at[r ^ via, side], r)
    number, _ = number_of(brick, partner(high))
    incoming[high, upper] = stage[0, number]
    number, _ = number_of(brick, partner(low))
    incoming[low, lower] = stage[1, number]

    arrivals = (
        (0, ()), (1, (2,)), (low, (3,)), (high, (5,)), (low + 1, (4, 12)), (high + 1, (6, 11)),
        (low + high, (7, 9)), (low + high + 1, (8, 10)),
    )
    density = jnp.zeros((1, points), jnp.float32)
    for step, (r, needs) in enumerate(arrivals):
        where, taken = position_in(crossing_ref, own, brick, partner(r) if r else brick)
        for n in needs:
            sends[n].wait_recv()
        product = jnp.dot(incoming[r], col_t[where], preferred_element_type=jnp.float32)
        term = jnp.sum(row_t[where].astype(jnp.float32) * product, axis=0, keepdims=True)
        density = density + jnp.where(taken == 1, term, 0.0)
        if step < len(arrivals) - 1:
            spread(step + 2)
    for n in range(len(arrivals) + 1, groups):
        spread(n)
    for x in range(tall):
        dens[x : x + 1, :] = density[:, x * wide : (x + 1) * wide]
    around = [(dg, db) for dg in (-1, 0, 1) for db in (-1, 0, 1) if (dg, db) != (0, 0)]
    exchange = []
    for n, (dg, db) in enumerate(around):
        target = (lax.rem(group + dg % groups, groups), lax.rem(brick + db % bricks, bricks))
        copy = pltpu.make_async_remote_copy(
            src_ref=dens, dst_ref=halo.at[1 - dg, 1 - db],
            send_sem=halo_send.at[n], recv_sem=halo_recv.at[n],
            device_id=target, device_id_type=MESH,
        )
        copy.start()
        exchange.append(copy)
    halo[1, 1] = dens[...]
    for n in sends:
        sends[n].wait_send()
    for copy in exchange:
        copy.wait()
    scaled = scaled_potential(halo, size_z)

    def partial_of(r):
        where, _ = position_in(crossing_ref, own, brick, partner(r) if r else brick)
        weighted = (col_t[where].astype(jnp.float32) * scaled).astype(jnp.bfloat16)
        return lax.dot_general(row_t[where], weighted, NT, preferred_element_type=jnp.float32)

    give = sender(back_send, back_recv)
    returns = {}
    routes = {
        low + high: ((0, upper, relay.at[0, 1], low), (2, lower, relay.at[1, 1], high)),
        low + high + 1: ((1, upper, relay.at[0, 2], low + 1), (3, lower, relay.at[1, 2], high + 1)),
        high + 1: ((6, lower, direct.at[3], high + 1), (4, upper, relay.at[0, 0], 1)),
        low + 1: ((7, upper, direct.at[1], low + 1), (5, lower, relay.at[1, 0], 1)),
        low: ((8, upper, direct.at[0], low),),
        high: ((9, lower, direct.at[2], high),),
    }
    for r, ways in routes.items():
        value = partial_of(r)
        back[r] = value.astype(jnp.bfloat16)
        if r == low:
            kept[1] = value[half:]
        if r == high:
            kept[0] = value[:half]
        for n, side, target, over in ways:
            returns[n] = give(n, back.at[r, side], target, over)
    back[1] = partial_of(1).astype(jnp.bfloat16)
    returns[10] = give(10, back.at[1], mate_back, 1)
    value = partial_of(0)
    number, taken = number_of(brick, brick)
    for k in range(own):
        total_v[k] = jnp.where((taken == 1) & (number == k), value, 0.0)

    for n in range(6):
        returns[n].wait_recv()
    first = 11
    for k in range(own):
        for side, via, other in ((0, high, low), (1, low, high)):
            total = jnp.zeros((half, width), jnp.float32)
            for n, r in enumerate((0, 1, other, other + 1)):
                number, taken = number_of(partner(r) if r else brick, partner(via))
                value = relay[side, n - 1].astype(jnp.float32) if n else kept[side]
                total = total + jnp.where((taken == 1) & (number == k), value, 0.0)
            sums[side, k] = total.astype(jnp.bfloat16)
            n = first + 2 * k + side
            returns[n] = give(n, sums.at[side, k], far_hbm.at[k, upper if side == 0 else lower], via)

    for n in range(6, first):
        returns[n].wait_recv()
    for side, rows, other in ((0, upper, low), (1, lower, high)):
        pieces = []
        for r in (1, other, other + 1):
            number, taken = number_of(partner(r), brick)
            value = mate_back[rows] if r == 1 else direct[2 * side + r - other]
            pieces.append((number, taken, value.astype(jnp.float32)))
        for k in range(own):
            total = total_v[k, rows]
            for number, taken, value in pieces:
                total = total + jnp.where((taken == 1) & (number == k), value, 0.0)
            total_v[k, rows] = total
    keep = pltpu.make_async_copy(total_v, near_hbm, near_sem)
    keep.start()
    keep.wait()
    for n in range(first, first + 2 * own):
        returns[n].wait_recv()
    for n in returns:
        returns[n].wait_send()


def cube_call(groups, bricks, store, crossing, phi, rows_index, cols_index):
    own, width = store.shape[0], store.shape[1]
    blocks = crossing.shape[0]
    size_x, size_y, size_z, functions = phi.shape
    points = size_x * size_y * size_z
    tall, wide = size_x, size_y * size_z
    half = width // 2
    hbm = pl.BlockSpec(memory_space=pl.ANY)
    tables = (blocks, width, points)
    back_copies = 11 + 2 * own
    near, far = pl.pallas_call(
        functools.partial(cube_kernel, groups, bricks, size_z),
        out_shape=[
            jax.ShapeDtypeStruct((own, width, width), jnp.float32),
            jax.ShapeDtypeStruct((own, width, width), jnp.bfloat16),
        ],
        in_specs=[pl.BlockSpec(memory_space=pltpu.SMEM), hbm, hbm, hbm, hbm],
        out_specs=[hbm, hbm],
        scratch_shapes=[
            pltpu.VMEM(rows_index.shape, jnp.int32),
            pltpu.VMEM(cols_index.shape, jnp.int32),
            pltpu.VMEM((own, width, width), jnp.bfloat16),
            pltpu.VMEM((points, functions), jnp.bfloat16),
            pltpu.VMEM((width, width), jnp.bfloat16),
            pltpu.VMEM((10, half, width), jnp.bfloat16),
            pltpu.VMEM((2, own, half, width), jnp.bfloat16),
            pltpu.VMEM((bricks, width, width), jnp.bfloat16),
            pltpu.VMEM(tables, jnp.bfloat16),
            pltpu.VMEM(tables, jnp.bfloat16),
            pltpu.VMEM((tall, wide), jnp.float32),
            pltpu.VMEM((3, 3, tall, wide), jnp.float32),
            pltpu.VMEM((bricks, width, width), jnp.bfloat16),
            pltpu.VMEM((2, half, width), jnp.float32),
            pltpu.VMEM((2, 3, half, width), jnp.bfloat16),
            pltpu.VMEM((2, own, half, width), jnp.bfloat16),
            pltpu.VMEM((4, half, width), jnp.bfloat16),
            pltpu.VMEM((width, width), jnp.bfloat16),
            pltpu.VMEM((own, width, width), jnp.float32),
            pltpu.SemaphoreType.DMA((4,)),
            pltpu.SemaphoreType.DMA,
            pltpu.SemaphoreType.DMA((13,)),
            pltpu.SemaphoreType.DMA((13,)),
            pltpu.SemaphoreType.REGULAR((groups,)),
            pltpu.SemaphoreType.DMA((8,)),
            pltpu.SemaphoreType.DMA((8,)),
            pltpu.SemaphoreType.DMA((back_copies,)),
            pltpu.SemaphoreType.DMA((back_copies,)),
        ],
        compiler_params=pltpu.CompilerParams(
            collective_id=0, has_side_effects=True, vmem_limit_bytes=60 << 20
        ),
    )(crossing, rows_index, cols_index, store, phi.reshape(points, functions))
    return near + far.astype(jnp.float32)


def local(groups, bricks, store, crossing, phi, rows_index, cols_index):
    own, width = store.shape[0], store.shape[1]
    crossing = crossing.T
    blocks = crossing.shape[0]
    size_x, size_y, size_z, functions = phi.shape
    points = size_x * size_y * size_z
    tall, wide = size_x, size_y * size_z
    slots = (bricks, width, width)
    if bricks == CORE * LOW * HIGH:
        return cube_call(groups, bricks, store, crossing, phi, rows_index, cols_index)
    return pl.pallas_call(
        functools.partial(kernel, groups, bricks, size_z),
        out_shape=jax.ShapeDtypeStruct((own, width, width), jnp.float32),
        in_specs=[
            pl.BlockSpec(memory_space=pltpu.SMEM),
            pl.BlockSpec(memory_space=pl.ANY),
            pl.BlockSpec(memory_space=pl.ANY),
            pl.BlockSpec(memory_space=pl.ANY),
            pl.BlockSpec(memory_space=pl.ANY),
        ],
        out_specs=pl.BlockSpec(memory_space=pltpu.VMEM),
        scratch_shapes=[
            pltpu.VMEM(rows_index.shape, jnp.int32),
            pltpu.VMEM(cols_index.shape, jnp.int32),
            pltpu.VMEM((own, width, width), jnp.bfloat16),
            pltpu.VMEM((points, functions), jnp.bfloat16),
            pltpu.VMEM(slots, jnp.bfloat16),
            pltpu.VMEM(slots, jnp.bfloat16),
            pltpu.VMEM((blocks, width, points), jnp.bfloat16),
            pltpu.VMEM((blocks, width, points), jnp.bfloat16),
            pltpu.VMEM((tall, wide), jnp.float32),
            pltpu.VMEM((3, 3, tall, wide), jnp.float32),
            pltpu.VMEM(slots, jnp.bfloat16),
            pltpu.VMEM(slots, jnp.bfloat16),
            pltpu.SemaphoreType.DMA((4,)),
            pltpu.SemaphoreType.DMA((bricks,)),
            pltpu.SemaphoreType.DMA((bricks,)),
            pltpu.SemaphoreType.DMA((8,)),
            pltpu.SemaphoreType.DMA((8,)),
            pltpu.SemaphoreType.DMA((bricks,)),
            pltpu.SemaphoreType.DMA((bricks,)),
        ],
        compiler_params=pltpu.CompilerParams(
            collective_id=0, has_side_effects=True, vmem_limit_bytes=60 << 20
        ),
    )(crossing, rows_index, cols_index, store, phi.reshape(points, functions))


def solution(mesh):
    in_specs = (
        P(("grp", "brick"), None, None),
        P("grp", None),
        P("grp", "brick", None, None),
        P(("grp", "brick"), None, None),
        P(("grp", "brick"), None, None),
    )
    out_specs = P(("grp", "brick"), None, None)
    body = functools.partial(local, mesh.shape["grp"], mesh.shape["brick"])
    return jax.shard_map(body, mesh=mesh, in_specs=in_specs, out_specs=out_specs, check_vma=False)
```
